256 devices in a mesh: hel: 8 (over y_hi, x), grid: 32 (over z, y_lo, core).
Axes of the slice: x: 4, y: 4 (y_hi: 2, y_lo: 2; y = y_hi * 2 + y_lo), z: 8, core: 2. Of those that a mesh axis runs over, the one named last changes fastest.
Arguments:
- phi_prev: float32 [16, 1536, 4096], P('hel', 'grid'), may hold values from -6 to 6
- phi_curr: float32 [16, 1536, 4096], P('hel', 'grid'), may hold values from -6 to 6
- helicity: int32 [16], replicated, may hold values from 0 to 18, as said below
- band: int32 [1536], P('grid'), may hold values from 0 to 47
- rotation: float32 [1536], P('grid'), may hold values from 0.2 to 0.8
- coupling: float32 [1536], P('grid'), may hold values from 0.3 to 1
- damping: float32 [4096], replicated, may hold values from 0.6 to 1
- potential: float32 [1536, 4096], P(None, 'grid'), may hold values from -0.6 to 0.6
- transform: bfloat16 [1536, 1536], P('grid'), may hold values from -0.15625 to 0.15625
- radial_long: float32 [128, 128], replicated, may hold values from -0.5 to 0.5
- radial_short: float32 [32, 32], replicated, may hold values from -1 to 1
Outputs:
- phi_next: float32 [16, 1536, 4096], P('hel', 'grid')
- phi_after: float32 [16, 1536, 4096], P('hel', 'grid')
The draws below stay inside these ranges and needn't reach their ends.
Inputs may be any that keep to these rules, and one draw needn't show every extreme that they name: `helicity`: starts at 0 and is strictly increasing over the blocks; neighbouring blocks differ by 1 or 2, by 2 at exactly 3 places.
All inputs are finite; a program needn't handle non-finite values.
Results may differ from the reference program's by a relative error of at most 0.0013.
Values may be sent and summed in bfloat16 or wider, within the bound.
No kernel may reach another device: no remote copies, remote signals or barrier semaphores. Data moves between devices by JAX's collectives and lax.ppermute only.
A program may use at most 128 MiB of HBM per device.

```python
import math
import jax
import jax.numpy as jnp
from jax import lax

NR = 128
NS = 32
ANG = 1536
JMAX = 48
HELICITY = 16
CELLS = 4096


def draw_helicity(key, part):
    order = jax.random.permutation(jax.random.fold_in(key, 12), HELICITY - 1)
    increments = 1 + (order < (HELICITY - 1) // 4).astype(jnp.int32)
    first = jnp.zeros((1,), jnp.int32)
    return jnp.concatenate([first, jnp.cumsum(increments).astype(jnp.int32)]).astype(jnp.int32)


def set_ends(result, rng, smallest, high):
    shape = result.shape
    spot = [jax.random.randint(jax.random.fold_in(rng, axis), (), 0, shape[axis]) for axis in range(len(shape))]
    result = result.at[tuple(spot)].set(smallest)
    longest = shape.index(max(shape))
    spot[longest] = (spot[longest] + 1) % shape[longest]
    return result.at[tuple(spot)].set(high)


def steps_of(rng, extent, cuts, smallest, largest):
    gain, own = 1.0, jax.random.fold_in(rng, 6)
    for position, shards_of in cuts:
        heights = jnp.exp(jax.random.uniform(jax.random.fold_in(own, position), (shards_of,), jnp.float32, smallest / len(cuts), largest / len(cuts)))
        gain = gain * jnp.repeat(heights, extent[position] // shards_of).reshape([-1 if axis == position else 1 for axis in range(len(extent))])
    return gain


def normal_values(stream_key, extent, spread, most, pieces=(), held_as=jnp.bfloat16):
    values = spread * jax.random.normal(stream_key, extent, jnp.float32)
    if pieces:
        values = values * steps_of(stream_key, extent, pieces, -0.22, 0.18)
    return jnp.clip(values, -most, most).astype(held_as)


def setup_inputs(seed: int = 0) -> dict:
    key_of = jax.random.split(jax.random.key(seed), 12)
    return {
        "phi_prev": normal_values(key_of[0], (HELICITY, ANG, CELLS), 1.0, 6.0, ((0, 8), (1, 32)), jnp.float32),
        "phi_curr": normal_values(key_of[1], (HELICITY, ANG, CELLS), 1.0, 6.0, ((0, 8), (1, 32)), jnp.float32),
        "helicity": draw_helicity(jax.random.fold_in(key_of[11], 71), 0),
        "band": set_ends(jax.random.randint(key_of[3], (ANG,), 0, JMAX), jax.random.fold_in(key_of[3], 1), 0, JMAX - 1).astype(jnp.int32),
        "rotation": jnp.clip(jnp.exp(math.log(0.8) - 1.3862944 * jax.random.uniform(key_of[4], (ANG,), jnp.float32) ** steps_of(key_of[4], (ANG,), ((0, 32),), -0.2, 0.2)), 0.2, 0.8),
        "coupling": jnp.clip(0.3 + 0.7 * jax.random.uniform(key_of[5], (ANG,), jnp.float32) ** steps_of(key_of[5], (ANG,), ((0, 32),), -0.2, 0.2), 0.3, 1.0),
        "damping": jnp.clip(jax.random.uniform(key_of[6], (CELLS,), jnp.float32, 0.6, 1.0), 0.6, 1.0),
        "potential": jnp.clip(jax.random.uniform(key_of[7], (ANG, CELLS), jnp.float32, -0.6, 0.6) * steps_of(key_of[7], (ANG, CELLS), ((1, 32),), -0.4, 0.0), -0.6, 0.6),
        "transform": normal_values(key_of[8], (ANG, ANG), ANG ** -0.5, 0.15625, ((0, 32),)),
        "radial_long": normal_values(key_of[9], (NR, NR), NR ** -0.5, 0.5, (), jnp.float32),
        "radial_short": normal_values(key_of[10], (NS, NS), NS ** -0.5, 1.0, (), jnp.float32),
    }


def symmetric(matrix):
    return 0.5 * (matrix + matrix.T)

def reference(phi_prev, phi_curr, helicity, band, rotation, coupling, damping, potential, transform, radial_long, radial_short):
    long_kin = symmetric(radial_long)
    short_kin = symmetric(radial_short)
    quantum = band.astype(jnp.float32)
    j_term = quantum * (quantum + 1.0)
    k_values = helicity.astype(jnp.float32)
    angular = rotation[None, :] * (j_term[None, :] - 2.0 * k_values[:, None] * k_values[:, None]) / (JMAX * JMAX)
    base = jnp.sqrt(jnp.maximum(j_term[None, :] - (k_values * (k_values + 1.0))[:, None], 0.0)) / JMAX
    linked = (helicity[1:] - helicity[:-1] == 1).astype(jnp.float32)
    linked = jnp.concatenate([linked, jnp.zeros((1,), jnp.float32)])
    coriolis = coupling[None, :] * base * linked[:, None]
    shifted = jnp.concatenate([jnp.zeros_like(coriolis[:1]), coriolis[:-1]], axis=0)
    table = transform.astype(jnp.float32)

    def block_part(packet):
        shaped = packet.reshape(ANG, NR, NS)
        kinetic = jnp.einsum('ij,bjm->bim', long_kin, shaped, precision=lax.Precision.HIGHEST)
        kinetic = kinetic + jnp.einsum('mn,bin->bim', short_kin, shaped, precision=lax.Precision.HIGHEST)
        kinetic = kinetic.reshape(ANG, CELLS)
        rounded = lax.optimization_barrier(packet.astype(jnp.bfloat16)).astype(jnp.float32)
        on_grid = jnp.dot(table, rounded, precision=lax.Precision.HIGHEST)
        weighted = lax.optimization_barrier((potential * on_grid).astype(jnp.bfloat16)).astype(jnp.float32)
        summed = jnp.dot(table.T, weighted, precision=lax.Precision.HIGHEST)
        returned = lax.optimization_barrier(summed.astype(jnp.bfloat16)).astype(jnp.float32)
        return (kinetic, returned)

    def hamiltonian(packet):
        kinetic, returned = lax.map(block_part, packet)
        empty = jnp.zeros_like(packet[:1])
        above = jnp.concatenate([packet[1:], empty], axis=0)
        below = jnp.concatenate([empty, packet[:-1]], axis=0)
        coupled = coriolis[:, :, None] * above + shifted[:, :, None] * below
        return kinetic + angular[:, :, None] * packet + coupled + returned
    phi_next = damping * (2.0 * hamiltonian(phi_curr) - damping * phi_prev)
    phi_after = damping * (2.0 * hamiltonian(phi_next) - damping * phi_curr)
    return (phi_next, phi_after)
```

```python
import functools
import jax
import jax.numpy as jnp
from jax import lax
from jax.experimental import pallas as pl
from jax.experimental.pallas import tpu as pltpu
from jax.sharding import Mesh, PartitionSpec as P

JMAX = 48
HEL = ("y_hi", "x")
GRID = ("z", "y_lo", "core")
VMEM = pl.BlockSpec(memory_space=pltpu.VMEM)
SMEM = pl.BlockSpec(memory_space=pltpu.SMEM)
PARAMS = pltpu.CompilerParams(vmem_limit_bytes=48 << 20)
F32, BF16, F16 = jnp.float32, jnp.bfloat16, jnp.float16


def split(x):
    high = x.astype(BF16)
    return high, (x - high.astype(F32)).astype(BF16)


def dot(a, b):
    return jnp.dot(a, b, preferred_element_type=F32)


def pack(v, dtype):
    return v.astype(dtype).reshape(2, 48, 32, 128).transpose(2, 0, 1, 3).reshape(32, 96, 128)


def local_kernel(prev_ref, coef_ref, damp_ref, long_ref, short_ref, *refs):
    if len(refs) == 4:
        (v_ref, out_ref, z_ref, y_ref), pot_ref = refs, None
    else:
        base_ref, pot_ref, v_ref, out_ref, z_ref, y_ref = refs

    def load(k, j):
        at = pl.ds(pl.multiple_of(j * 128, 128), 128)
        if pot_ref is None:
            return v_ref[k, :, at]
        pot = pot_ref[j, 48 * k : 48 * k + 48, :].astype(F32)
        v = base_ref[k, :, at] + 2.0 * damp_ref[:, at] * pot
        v_ref[k, :, at] = v
        return v

    def halves(ref):
        high, low = split(0.5 * (ref[...] + ref[...].T))
        top = jnp.concatenate([high, high], axis=1)
        return jnp.concatenate([top, jnp.concatenate([low, jnp.zeros_like(low)], axis=1)], axis=0)

    long_kin, short_kin = halves(long_ref), halves(short_ref)
    pad = jnp.zeros((32, 128), F32)

    def times(kin, one, two):
        high, low = split(jnp.concatenate([one, two], axis=1))
        both = dot(kin, jnp.concatenate([high, low], axis=0))
        return both[0:128] + both[128:256]

    def first(i, _):
        z = []
        for n in range(2):
            at = pl.ds(pl.multiple_of(i * 256 + n * 128, 128), 128)
            z.append(jnp.concatenate([load(0, 2 * i + n), load(1, 2 * i + n), pad], axis=0).T)
            z_ref[at, :] = z[n]
        y = times(short_kin, *z)
        for n in range(2):
            at = pl.ds(pl.multiple_of(i * 256 + n * 128, 128), 128)
            y_ref[at, :] = y[:, 128 * n : 128 * n + 128]
        return 0

    lax.fori_loop(0, 16, first, 0, unroll=4)

    def second(m, _):
        at = [pl.ds(2 * m + n, 128, stride=32) for n in range(2)]
        y = times(long_kin, z_ref[at[0], :], z_ref[at[1], :])
        for n in range(2):
            y_ref[at[n], :] = y_ref[at[n], :] + y[:, 128 * n : 128 * n + 128]
        return 0

    lax.fori_loop(0, 16, second, 0, unroll=4)

    def third(i, _):
        at = pl.ds(pl.multiple_of(i * 128, 128), 128)
        kinetic = y_ref[at, :].T
        damp = damp_ref[:, at]
        v0, v1 = v_ref[0, :, at], v_ref[1, :, at]
        h0 = kinetic[0:48] + coef_ref[:, 0:1] * v0 + coef_ref[:, 2:3] * v1
        h1 = kinetic[48:96] + coef_ref[:, 1:2] * v1 + coef_ref[:, 3:4] * v0
        out_ref[0, :, at] = damp * (2.0 * h0 - damp * prev_ref[0, :, at])
        out_ref[1, :, at] = damp * (2.0 * h1 - damp * prev_ref[1, :, at])
        return 0

    lax.fori_loop(0, 32, third, 0, unroll=4)


SCRATCH = [pltpu.VMEM((4096, 128), F32)] * 2


def local_part(v, prev, coef, damp, radial_long, short_four):
    return pl.pallas_call(
        local_kernel,
        in_specs=[VMEM] * 6,
        out_specs=VMEM,
        out_shape=jax.ShapeDtypeStruct(v.shape, F32),
        scratch_shapes=SCRATCH,
        compiler_params=PARAMS,
        name="local_part",
    )(prev, coef, damp, radial_long, short_four, v)


def next_part(base, pot, prev, coef, damp, radial_long, short_four):
    return pl.pallas_call(
        local_kernel,
        in_specs=[VMEM] * 7,
        out_specs=[VMEM, VMEM],
        out_shape=[jax.ShapeDtypeStruct(base.shape, F32)] * 2,
        scratch_shapes=SCRATCH,
        compiler_params=PARAMS,
        name="next_part",
    )(prev, coef, damp, radial_long, short_four, base, pot)


def add_halo(part, below, above, coef, damp):
    beside = jnp.concatenate([coef[None, :, 4:5] * below, coef[None, :, 5:6] * above], axis=0)
    return part + 2.0 * damp * beside


def last_kernel(part_ref, below_ref, above_ref, pot_ref, coef_ref, damp_ref, out_ref):
    for j in range(pot_ref.shape[0]):
        at = pl.ds(128 * j, 128)
        two_damp = 2.0 * damp_ref[:, at]
        pot0 = pot_ref[j, 0:48, :].astype(F32) + coef_ref[:, 4:5] * below_ref[j]
        pot1 = pot_ref[j, 48:96, :].astype(F32) + coef_ref[:, 5:6] * above_ref[j]
        out_ref[0, :, at] = part_ref[0, :, at] + two_damp * pot0
        out_ref[1, :, at] = part_ref[1, :, at] + two_damp * pot1


def add_last(part, below, above, pot, coef, damp):
    step = 8
    wide = pl.BlockSpec((2, 48, 128 * step), lambda i: (0, 0, i))
    half = pl.BlockSpec((step, 48, 128), lambda i: (i, 0, 0))
    packed = pl.BlockSpec((step, 96, 128), lambda i: (i, 0, 0))
    coefs = pl.BlockSpec((48, 8), lambda i: (0, 0))
    damps = pl.BlockSpec((1, 128 * step), lambda i: (0, i))
    return pl.pallas_call(
        last_kernel,
        grid=(32 // step,),
        in_specs=[wide, half, half, packed, coefs, damps],
        out_specs=wide,
        out_shape=jax.ShapeDtypeStruct(part.shape, F32),
        name="add_last",
    )(part, below, above, pot, coef, damp)


def place(c, y, x, p, i):
    far = 1 if p in (1, 2) else 0
    across = (0, -1, 0, -1, 1, 2, 1, 2)[2 * p + i]
    rows = jnp.where(c == 0, abs(y - far), abs(y - i))
    columns = jnp.where(c == 0, x + across + 4, x + (0, -1, 1, 2)[p] + 4)
    return lax.rem(rows, 2), lax.rem(columns, 4)


def grid_kernel(where_ref, *refs):
    blocks_of, (v_ref, pot_ref, out_ref, x_ref, g_ref, w_ref, o_ref) = refs[:8], refs[8:]
    y, core, x = (where_ref[i] for i in range(3))
    for k in range(2):
        x_ref[:, 128 * k : 128 * k + 128] = v_ref[:, 48 * k : 48 * k + 48, :].reshape(1536, 128)
    g_ref[...] = jnp.zeros_like(g_ref)
    o_ref[...] = jnp.zeros_like(o_ref)
    todo = []
    for n in range(8):
        c = core if n < 4 else 1 - core
        for i in range(2):
            rows, columns = place(c, y, x, n % 4, i)
            todo.append((blocks_of[n], i, 2 * rows + c, columns))
    for ref, i, group, columns in todo:
        part = x_ref[pl.ds(pl.multiple_of(384 * columns, 384), 384), :]
        g_ref[group] = g_ref[group] + dot(ref[i], part)
    for group in range(4):
        pot = pot_ref[:, group].reshape(384, 128)
        weighted = jnp.concatenate([pot, pot], axis=1) * g_ref[group]
        w_ref[group] = weighted.T.astype(BF16)
    for ref, i, group, columns in todo:
        o_ref[columns] = o_ref[columns] + dot(w_ref[group], ref[i])
    for columns in range(4):
        back = o_ref[columns].T.astype(BF16)
        for k in range(2):
            out_ref[8 * columns : 8 * columns + 8, 48 * k : 48 * k + 48, :] = back[
                :, 128 * k : 128 * k + 128
            ].reshape(8, 48, 128)


def on_cells(where, table, v, pot):
    return pl.pallas_call(
        grid_kernel,
        in_specs=[SMEM] + [VMEM] * 10,
        out_specs=VMEM,
        out_shape=jax.ShapeDtypeStruct((32, 96, 128), BF16),
        scratch_shapes=[
            pltpu.VMEM((1536, 256), BF16),
            pltpu.VMEM((4, 384, 256), F32),
            pltpu.VMEM((4, 256, 384), BF16),
            pltpu.VMEM((4, 256, 384), F32),
        ],
        compiler_params=PARAMS,
        name="on_cells",
    )(where, *table, v, pot)


PLANE = ("x", "y_lo", "core")


def plane_permute(value, moves):
    pairs = []
    for x in range(4):
        for y in range(2):
            for c, move in enumerate(moves):
                if move is None:
                    continue
                to_x, to_y = ((x + move) % 4, y) if move else (x, 1 - y)
                pairs.append((4 * x + 2 * y + c, 4 * to_x + 2 * to_y + c))
    return lax.ppermute(value, PLANE, pairs)


def over_z(transform):
    columns = transform.shape[1] // 4
    block = lax.dynamic_slice_in_dim(transform, columns * lax.axis_index("x"), columns, 1)
    block = jnp.broadcast_to(block[None], (8,) + block.shape)
    return lax.all_to_all(block, "z", split_axis=0, concat_axis=0, tiled=True)


def over_plane_first(block):
    block = block.reshape(384, 384)
    one = plane_permute(block, (1, 0))
    two = plane_permute(block, (-1, None))
    three = plane_permute(block, (2, None))
    return jnp.stack([block, one]), jnp.stack([two, three])


def over_plane_second(near, far):
    first = lax.axis_index("core") == 0
    second = plane_permute(near, (0, 1))
    third = plane_permute(jnp.where(first, far, near), (0, -1))
    fourth = plane_permute(near, (None, 2))
    return second, third, fourth


def over_cores(near, far, second, third, fourth):
    first = lax.axis_index("core") == 0
    mine = [near, second, third, jnp.where(first, far, fourth)]
    return mine + [lax.ppermute(pair, "core", [(0, 1), (1, 0)]) for pair in mine]


def regroup(x):
    return lax.all_to_all(x, GRID, split_axis=0, concat_axis=0, tiled=True)


def halos(first, last):
    size = 8
    up = [(i, i + 1) for i in range(size - 1)]
    down = [(j, i) for i, j in up]
    return lax.ppermute(last, HEL, up), lax.ppermute(first, HEL, down)


def coefficients(helicity, band, rotation, coupling):
    first = 2 * lax.axis_index(HEL)
    quantum = band.astype(F32)
    j_term = quantum * (quantum + 1.0)
    k_values = helicity.astype(F32)
    base = jnp.sqrt(jnp.maximum(j_term[:, None] - (k_values * (k_values + 1.0))[None, :], 0.0)) / JMAX
    linked = (helicity[1:] - helicity[:-1] == 1).astype(F32)
    linked = jnp.concatenate([linked, jnp.zeros((1,), F32)])
    coriolis = coupling[:, None] * base * linked[None, :]
    angular = rotation[:, None] * (j_term[:, None] - 2.0 * k_values * k_values) / (JMAX * JMAX)
    padded = jnp.concatenate([jnp.zeros_like(coriolis[:, :1]), coriolis], axis=1)
    part = lax.dynamic_slice_in_dim(padded, first, 3, 1)
    angular = lax.dynamic_slice_in_dim(angular, first, 2, 1)
    return jnp.concatenate(
        [angular, part[:, 1:2], part[:, 1:2], part[:, 0:1], part[:, 2:3], part[:, 0:2]], axis=1
    )


def local(
    phi_prev, phi_curr, helicity, band, rotation, coupling, damping, potential, transform, radial_long, radial_short
):
    where = jnp.stack([lax.axis_index(name) for name in ("y_lo", "core", "x")]).astype(jnp.int32)
    coef = coefficients(helicity, band, rotation, coupling)
    damp = damping.reshape(1, -1)
    cell_damp = lax.dynamic_slice_in_dim(damp, 128 * lax.axis_index(GRID), 128, 1)
    short_four = jnp.kron(jnp.eye(4, dtype=F32), radial_short)
    pot_cells = potential.reshape(8, 4, 48, 128)

    block = over_z(transform)
    sent = pack(phi_curr, BF16)
    ends = (8192.0 * phi_curr).astype(F16)
    first, last = ends[0:1], ends[1:2]
    below, above = halos(first, last)
    v, sent, first, last = lax.optimization_barrier((phi_curr, sent, first, last))
    part = local_part(v, phi_prev, coef, damp, radial_long, short_four)
    sent, block, part = lax.optimization_barrier((sent, block, part))
    by_cells = regroup(sent)
    near, far = over_plane_first(block)
    second = over_plane_second(near, far)
    base = add_halo(part, below.astype(F32) / 8192, above.astype(F32) / 8192, coef, damp)
    sent, second = lax.optimization_barrier((pack(32.0 * base, F16), second))
    base_cells = regroup(sent)
    below, above = halos(sent[:, :48], sent[:, 48:])
    table = over_cores(near, far, *second)
    pot = on_cells(where, table, by_cells, pot_cells)
    next_cells = base_cells.astype(F32) / 32 + 2.0 * cell_damp * pot.astype(F32)
    pot, below, above = lax.optimization_barrier((pot, below, above))
    pot_back = regroup(pot)
    pot_after = on_cells(where, table, next_cells.astype(BF16), pot_cells)
    pot_below, pot_above = halos(pot_back[:, :48], pot_back[:, 48:])
    phi_next, part = next_part(base, pot_back, phi_curr, coef, damp, radial_long, short_four)
    two_damp = 2.0 * damp.reshape(32, 1, 128)
    below = below.astype(F32) / 32 + two_damp * pot_below.astype(F32)
    above = above.astype(F32) / 32 + two_damp * pot_above.astype(F32)
    phi_after = add_last(part, below, above, regroup(pot_after), coef, damp)
    return phi_next, phi_after


def solution(mesh):
    inner = Mesh(mesh.devices.reshape(2, 4, 8, 2, 2), HEL + GRID)
    in_specs = (
        P(HEL, GRID, None),
        P(HEL, GRID, None),
        P(),
        P(GRID),
        P(GRID),
        P(GRID),
        P(),
        P(None, GRID),
        P(GRID, None),
        P(),
        P(),
    )
    out_specs = (P(HEL, GRID, None), P(HEL, GRID, None))
    return jax.shard_map(local, mesh=inner, in_specs=in_specs, out_specs=out_specs, check_vma=False)
```

```python
import functools
import jax
import jax.numpy as jnp
from jax import lax
from jax.experimental import pallas as pl
from jax.experimental.pallas import tpu as pltpu
from jax.sharding import Mesh, PartitionSpec as P

JMAX = 48
HEL = ("y_hi", "x")
GRID = ("z", "y_lo", "core")
VMEM = pl.BlockSpec(memory_space=pltpu.VMEM)
SMEM = pl.BlockSpec(memory_space=pltpu.SMEM)
PARAMS = pltpu.CompilerParams(vmem_limit_bytes=48 << 20)
F32, BF16, F16 = jnp.float32, jnp.bfloat16, jnp.float16


def split(x):
    high = x.astype(BF16)
    return high, (x - high.astype(F32)).astype(BF16)


def dot(a, b):
    return jnp.dot(a, b, preferred_element_type=F32)


def pack(v):
    return v.reshape(48, 32, 128).transpose(1, 0, 2)


def local_kernel(prev_ref, coef_ref, damp_ref, long_ref, short_ref, *refs):
    if len(refs) == 5:
        (v_ref, out_ref, rounded_ref, z_ref, y_ref), pot_ref = refs, None
    else:
        base_ref, pot_ref, v_ref, out_ref, z_ref, y_ref = refs

    def load(k, j):
        at = pl.ds(pl.multiple_of(j * 128, 128), 128)
        rows = slice(48 * k, 48 * k + 48)
        if pot_ref is None:
            rounded_ref[j, rows, :] = v_ref[k, :, at].astype(BF16)
            return v_ref[k, :, at]
        v = base_ref[j, rows, :] + 2.0 * damp_ref[:, at] * pot_ref[j, rows, :].astype(F32)
        v_ref[k, :, at] = v
        return v

    def halves(matrix):
        high, low = split(0.5 * (matrix + matrix.T))
        top = jnp.concatenate([high, high], axis=1)
        return jnp.concatenate([top, jnp.concatenate([low, jnp.zeros_like(low)], axis=1)], axis=0)

    row, column = (lax.broadcasted_iota(jnp.int32, (128, 128), axis) // 32 for axis in range(2))
    short = jnp.concatenate([short_ref[...]] * 4, axis=1)
    short = jnp.where(row == column, jnp.concatenate([short] * 4, axis=0), 0.0)
    long_kin, short_kin = halves(long_ref[...]), halves(short)
    pad = jnp.zeros((32, 128), F32)

    def times(kin, one, two):
        high, low = split(jnp.concatenate([one, two], axis=1))
        both = dot(kin, jnp.concatenate([high, low], axis=0))
        return both[0:128] + both[128:256]

    def first(i, _):
        z = []
        for n in range(2):
            at = pl.ds(pl.multiple_of(i * 256 + n * 128, 128), 128)
            z.append(jnp.concatenate([load(0, 2 * i + n), load(1, 2 * i + n), pad], axis=0).T)
            z_ref[at, :] = z[n]
        y = times(short_kin, *z)
        for n in range(2):
            at = pl.ds(pl.multiple_of(i * 256 + n * 128, 128), 128)
            y_ref[at, :] = y[:, 128 * n : 128 * n + 128]
        return 0

    lax.fori_loop(0, 16, first, 0, unroll=4)

    def second(m, _):
        at = [pl.ds(2 * m + n, 128, stride=32) for n in range(2)]
        y = times(long_kin, z_ref[at[0], :], z_ref[at[1], :])
        for n in range(2):
            y_ref[at[n], :] = y_ref[at[n], :] + y[:, 128 * n : 128 * n + 128]
        return 0

    lax.fori_loop(0, 16, second, 0, unroll=4)

    def third(i, _):
        at = pl.ds(pl.multiple_of(i * 128, 128), 128)
        kinetic = y_ref[at, :].T
        damp = damp_ref[:, at]
        v0, v1 = v_ref[0, :, at], v_ref[1, :, at]
        h0 = kinetic[0:48] + coef_ref[:, 0:1] * v0 + coef_ref[:, 2:3] * v1
        h1 = kinetic[48:96] + coef_ref[:, 1:2] * v1 + coef_ref[:, 3:4] * v0
        out_ref[i, 0:48, :] = damp * (2.0 * h0 - damp * prev_ref[0, :, at])
        out_ref[i, 48:96, :] = damp * (2.0 * h1 - damp * prev_ref[1, :, at])
        return 0

    lax.fori_loop(0, 32, third, 0, unroll=4)


PACKED = jax.ShapeDtypeStruct((32, 96, 128), F32)
SCRATCH = [pltpu.VMEM((4096, 128), F32)] * 2


def local_part(v, prev, coef, damp, radial_long, radial_short):
    return pl.pallas_call(
        local_kernel,
        in_specs=[VMEM] * 6,
        out_specs=[VMEM, VMEM],
        out_shape=[PACKED, jax.ShapeDtypeStruct(PACKED.shape, BF16)],
        scratch_shapes=SCRATCH,
        compiler_params=PARAMS,
        name="local_part",
    )(prev, coef, damp, radial_long, radial_short, v)


def next_part(base, pot, prev, coef, damp, radial_long, radial_short):
    return pl.pallas_call(
        local_kernel,
        in_specs=[VMEM] * 7,
        out_specs=[VMEM, VMEM],
        out_shape=[jax.ShapeDtypeStruct(prev.shape, F32), PACKED],
        scratch_shapes=SCRATCH,
        compiler_params=PARAMS,
        name="next_part",
    )(prev, coef, damp, radial_long, radial_short, base, pot)


def last_kernel(part_ref, below_ref, above_ref, pot_ref, coef_ref, damp_ref, out_ref):
    for j in range(pot_ref.shape[0]):
        at = pl.ds(128 * j, 128)
        two_damp = 2.0 * damp_ref[:, at]
        pot0 = pot_ref[j, 0:48, :].astype(F32) + coef_ref[:, 4:5] * below_ref[j]
        pot1 = pot_ref[j, 48:96, :].astype(F32) + coef_ref[:, 5:6] * above_ref[j]
        out_ref[0, :, at] = part_ref[j, 0:48, :] + two_damp * pot0
        out_ref[1, :, at] = part_ref[j, 48:96, :] + two_damp * pot1


def add_last(part, below, above, pot, coef, damp):
    step = 8
    wide = pl.BlockSpec((2, 48, 128 * step), lambda i: (0, 0, i))
    half = pl.BlockSpec((step, 48, 128), lambda i: (i, 0, 0))
    packed = pl.BlockSpec((step, 96, 128), lambda i: (i, 0, 0))
    coefs = pl.BlockSpec((48, 8), lambda i: (0, 0))
    damps = pl.BlockSpec((1, 128 * step), lambda i: (0, i))
    return pl.pallas_call(
        last_kernel,
        grid=(32 // step,),
        in_specs=[packed, half, half, packed, coefs, damps],
        out_specs=wide,
        out_shape=jax.ShapeDtypeStruct((2, 48, 4096), F32),
        name="add_last",
    )(part, below, above, pot, coef, damp)


ACROSS = (0, -1, 1, 2)


def grid_kernel(where_ref, own_ref, own_far_ref, other_ref, other_far_ref, v_ref, pot_ref, out_ref, x_ref, w_ref):
    y, core, x = (where_ref[i] for i in range(3))
    owners = [pl.ds(8 * lax.rem(x + across + 4, 4), 8) for across in ACROSS]
    for i, owner in enumerate(owners):
        for k in range(2):
            part = v_ref[owner, 48 * k : 48 * k + 48, :].reshape(384, 128)
            x_ref[384 * i : 384 * i + 384, 128 * k : 128 * k + 128] = part
    halves = (own_ref, own_far_ref), (other_ref, other_far_ref)
    for n, (half, c) in enumerate(zip(halves, (core, 1 - core))):
        for m, (t_ref, rows) in enumerate(zip(half, (y, 1 - y))):
            on_grid = dot(t_ref[...], x_ref[...])
            pot = pot_ref[:, 2 * rows + c].reshape(384, 128)
            weighted = jnp.concatenate([pot, pot], axis=1) * on_grid
            at = 768 * n + 384 * m
            w_ref[:, at : at + 384] = weighted.T.astype(BF16)
    for i, owner in enumerate(owners):
        at = slice(384 * i, 384 * i + 384)
        summed = 0.0
        for n, half in enumerate(halves):
            t = jnp.concatenate([t_ref[:, at] for t_ref in half], axis=0)
            summed = summed + dot(w_ref[:, 768 * n : 768 * n + 768], t)
        back = summed.T.astype(BF16)
        for k in range(2):
            out_ref[owner, 48 * k : 48 * k + 48, :] = back[:, 128 * k : 128 * k + 128].reshape(8, 48, 128)


def on_cells(where, table, v, pot):
    return pl.pallas_call(
        grid_kernel,
        in_specs=[SMEM] + [VMEM] * 6,
        out_specs=VMEM,
        out_shape=jax.ShapeDtypeStruct((32, 96, 128), BF16),
        scratch_shapes=[pltpu.VMEM((1536, 256), BF16), pltpu.VMEM((256, 1536), BF16)],
        compiler_params=PARAMS,
        name="on_cells",
    )(where, *table, v, pot)


def over_z(transform):
    columns = transform.shape[1] // 4
    block = lax.dynamic_slice_in_dim(transform, columns * lax.axis_index("x"), columns, 1)
    block = jnp.broadcast_to(block[None], (8,) + block.shape)
    return lax.all_to_all(block, "z", split_axis=0, concat_axis=0, tiled=True).reshape(-1, columns)


def over_x(block):
    return [lax.ppermute(block, "x", [(i, (i - across) % 4) for i in range(4)]) for across in ACROSS[1:]]


def over_plane(block):
    far = lax.ppermute(block, "y_lo", [(0, 1), (1, 0)])
    own, far, near = lax.optimization_barrier((block, far, over_x(block)))
    mine = jnp.concatenate([own] + near, axis=1)
    others = lax.optimization_barrier(over_x(far))
    mine = [mine, jnp.concatenate([far] + others, axis=1)]
    return mine + [lax.ppermute(rows, "core", [(0, 1), (1, 0)]) for rows in mine]


def regroup(x):
    return lax.all_to_all(x, GRID, split_axis=0, concat_axis=0, tiled=True)


def halos(first, last):
    size = 8
    up = [(i, i + 1) for i in range(size - 1)]
    down = [(j, i) for i, j in up]
    return lax.ppermute(last, HEL, up), lax.ppermute(first, HEL, down)


def coefficients(helicity, band, rotation, coupling):
    first = 2 * lax.axis_index(HEL)
    quantum = band.astype(F32)
    j_term = quantum * (quantum + 1.0)
    k_values = helicity.astype(F32)
    base = jnp.sqrt(jnp.maximum(j_term[:, None] - (k_values * (k_values + 1.0))[None, :], 0.0)) / JMAX
    linked = (helicity[1:] - helicity[:-1] == 1).astype(F32)
    linked = jnp.concatenate([linked, jnp.zeros((1,), F32)])
    coriolis = coupling[:, None] * base * linked[None, :]
    angular = rotation[:, None] * (j_term[:, None] - 2.0 * k_values * k_values) / (JMAX * JMAX)
    padded = jnp.concatenate([jnp.zeros_like(coriolis[:, :1]), coriolis], axis=1)
    part = lax.dynamic_slice_in_dim(padded, first, 3, 1)
    angular = lax.dynamic_slice_in_dim(angular, first, 2, 1)
    return jnp.concatenate(
        [angular, part[:, 1:2], part[:, 1:2], part[:, 0:1], part[:, 2:3], part[:, 0:2]], axis=1
    )


def local(
    phi_prev, phi_curr, helicity, band, rotation, coupling, damping, potential, transform, radial_long, radial_short
):
    where = jnp.stack([lax.axis_index(name) for name in ("y_lo", "core", "x")]).astype(jnp.int32)
    coef = coefficients(helicity, band, rotation, coupling)
    damp = damping.reshape(1, -1)
    cell_damp = lax.dynamic_slice_in_dim(damp, 128 * lax.axis_index(GRID), 128, 1)
    pot_cells = potential.reshape(8, 4, 48, 128)

    two_damp = 2.0 * damp.reshape(32, 1, 128)
    sides = jnp.concatenate([coef[:, 4], coef[:, 5]]).reshape(1, 96, 1)

    first, last = (pack((8192.0 * phi_curr[k]).astype(F16)) for k in range(2))
    below, above = lax.optimization_barrier(halos(first, last))
    block = over_z(transform)
    part, rounded = local_part(phi_curr, phi_prev, coef, damp, radial_long, radial_short)
    beside = jnp.concatenate([below, above], axis=1).astype(F32) / 8192
    sent = jnp.concatenate([(8192.0 * rounded.astype(F32)).astype(F16), (32.0 * (part + two_damp * (sides * beside))).astype(F16)], axis=1)
    sent, part, beside, _ = lax.optimization_barrier((sent, part, beside, block))
    by_cells = regroup(sent)
    base = part + two_damp * (sides * beside)
    table = over_plane(block)
    pot = on_cells(where, table, (by_cells[:, :96].astype(F32) / 8192).astype(BF16), pot_cells)
    next_cells = by_cells[:, 96:].astype(F32) / 32 + 2.0 * cell_damp * pot.astype(F32)
    pot_back = regroup(pot)
    pot_after = on_cells(where, table, next_cells.astype(BF16), pot_cells)
    first, last, pot_after = lax.optimization_barrier((sent[:, 96:144], sent[:, 144:], pot_after))
    below, above = halos(first, last)
    pot_below, pot_above = halos(pot_back[:, :48], pot_back[:, 48:])
    phi_next, part = next_part(base, pot_back, phi_curr, coef, damp, radial_long, radial_short)
    below = below.astype(F32) / 32 + two_damp * pot_below.astype(F32)
    above = above.astype(F32) / 32 + two_damp * pot_above.astype(F32)
    phi_after = add_last(part, below, above, regroup(pot_after), coef, damp)
    return phi_next, phi_after


def solution(mesh):
    inner = Mesh(mesh.devices.reshape(2, 4, 8, 2, 2), HEL + GRID)
    in_specs = (
        P(HEL, GRID, None),
        P(HEL, GRID, None),
        P(),
        P(GRID),
        P(GRID),
        P(GRID),
        P(),
        P(None, GRID),
        P(GRID, None),
        P(),
        P(),
    )
    out_specs = (P(HEL, GRID, None), P(HEL, GRID, None))
    return jax.shard_map(local, mesh=inner, in_specs=in_specs, out_specs=out_specs, check_vma=False)
```

```python
import functools
import jax
import jax.numpy as jnp
from jax import lax
from jax.experimental import pallas as pl
from jax.experimental.pallas import tpu as pltpu
from jax.sharding import Mesh, PartitionSpec as P

JMAX = 48
HEL = ("y_hi", "x")
GRID = ("z", "y_lo", "core")
VMEM = pl.BlockSpec(memory_space=pltpu.VMEM)
SMEM = pl.BlockSpec(memory_space=pltpu.SMEM)
PARAMS = pltpu.CompilerParams(vmem_limit_bytes=48 << 20)
F32, BF16, F16 = jnp.float32, jnp.bfloat16, jnp.float16


def split(x):
    high = x.astype(BF16)
    return high, (x - high.astype(F32)).astype(BF16)


def dot(a, b):
    return jnp.dot(a, b, preferred_element_type=F32)


def pack(v):
    return v.reshape(48, 32, 128).transpose(1, 0, 2)


def local_kernel(prev_ref, coef_ref, damp_ref, long_ref, short_ref, *refs):
    if len(refs) == 5:
        (v_ref, out_ref, rounded_ref, z_ref, y_ref), pot_ref = refs, None
    else:
        base_ref, pot_ref, v_ref, out_ref, z_ref, y_ref = refs

    def load(k, j):
        at = pl.ds(pl.multiple_of(j * 128, 128), 128)
        rows = slice(48 * k, 48 * k + 48)
        if pot_ref is None:
            rounded_ref[j, rows, :] = v_ref[k, :, at].astype(BF16)
            return v_ref[k, :, at]
        v = base_ref[j, rows, :] + 2.0 * damp_ref[:, at] * pot_ref[j, rows, :].astype(F32)
        v_ref[k, :, at] = v
        return v

    def halves(matrix):
        high, low = split(0.5 * (matrix + matrix.T))
        top = jnp.concatenate([high, high], axis=1)
        return jnp.concatenate([top, jnp.concatenate([low, jnp.zeros_like(low)], axis=1)], axis=0)

    row, column = (lax.broadcasted_iota(jnp.int32, (128, 128), axis) // 32 for axis in range(2))
    short = jnp.concatenate([short_ref[...]] * 4, axis=1)
    short = jnp.where(row == column, jnp.concatenate([short] * 4, axis=0), 0.0)
    long_kin, short_kin = halves(long_ref[...]), halves(short)
    pad = jnp.zeros((32, 128), F32)

    def times(kin, one, two):
        high, low = split(jnp.concatenate([one, two], axis=1))
        both = dot(kin, jnp.concatenate([high, low], axis=0))
        return both[0:128] + both[128:256]

    def first(i, _):
        z = []
        for n in range(2):
            at = pl.ds(pl.multiple_of(i * 256 + n * 128, 128), 128)
            z.append(jnp.concatenate([load(0, 2 * i + n), load(1, 2 * i + n), pad], axis=0).T)
            z_ref[at, :] = z[n]
        y = times(short_kin, *z)
        for n in range(2):
            at = pl.ds(pl.multiple_of(i * 256 + n * 128, 128), 128)
            y_ref[at, :] = y[:, 128 * n : 128 * n + 128]
        return 0

    lax.fori_loop(0, 16, first, 0, unroll=4)

    def second(m, _):
        at = [pl.ds(2 * m + n, 128, stride=32) for n in range(2)]
        y = times(long_kin, z_ref[at[0], :], z_ref[at[1], :])
        for n in range(2):
            y_ref[at[n], :] = y_ref[at[n], :] + y[:, 128 * n : 128 * n + 128]
        return 0

    lax.fori_loop(0, 16, second, 0, unroll=4)

    def third(i, _):
        at = pl.ds(pl.multiple_of(i * 128, 128), 128)
        kinetic = y_ref[at, :].T
        damp = damp_ref[:, at]
        v0, v1 = v_ref[0, :, at], v_ref[1, :, at]
        h0 = kinetic[0:48] + coef_ref[:, 0:1] * v0 + coef_ref[:, 2:3] * v1
        h1 = kinetic[48:96] + coef_ref[:, 1:2] * v1 + coef_ref[:, 3:4] * v0
        out_ref[i, 0:48, :] = damp * (2.0 * h0 - damp * prev_ref[0, :, at])
        out_ref[i, 48:96, :] = damp * (2.0 * h1 - damp * prev_ref[1, :, at])
        return 0

    lax.fori_loop(0, 32, third, 0, unroll=4)


PACKED = jax.ShapeDtypeStruct((32, 96, 128), F32)
SCRATCH = [pltpu.VMEM((4096, 128), F32)] * 2


def local_part(v, prev, coef, damp, radial_long, radial_short):
    return pl.pallas_call(
        local_kernel,
        in_specs=[VMEM] * 6,
        out_specs=[VMEM, VMEM],
        out_shape=[PACKED, jax.ShapeDtypeStruct(PACKED.shape, BF16)],
        scratch_shapes=SCRATCH,
        compiler_params=PARAMS,
        name="local_part",
    )(prev, coef, damp, radial_long, radial_short, v)


def next_part(base, pot, prev, coef, damp, radial_long, radial_short):
    return pl.pallas_call(
        local_kernel,
        in_specs=[VMEM] * 7,
        out_specs=[VMEM, VMEM],
        out_shape=[jax.ShapeDtypeStruct(prev.shape, F32), PACKED],
        scratch_shapes=SCRATCH,
        compiler_params=PARAMS,
        name="next_part",
    )(prev, coef, damp, radial_long, radial_short, base, pot)


def last_kernel(part_ref, below_ref, above_ref, pot_ref, coef_ref, damp_ref, out_ref):
    for j in range(pot_ref.shape[0]):
        at = pl.ds(128 * j, 128)
        two_damp = 2.0 * damp_ref[:, at]
        pot0 = pot_ref[j, 0:48, :].astype(F32) + coef_ref[:, 4:5] * below_ref[j]
        pot1 = pot_ref[j, 48:96, :].astype(F32) + coef_ref[:, 5:6] * above_ref[j]
        out_ref[0, :, at] = part_ref[j, 0:48, :] + two_damp * pot0
        out_ref[1, :, at] = part_ref[j, 48:96, :] + two_damp * pot1


def add_last(part, below, above, pot, coef, damp):
    step = 8
    wide = pl.BlockSpec((2, 48, 128 * step), lambda i: (0, 0, i))
    half = pl.BlockSpec((step, 48, 128), lambda i: (i, 0, 0))
    packed = pl.BlockSpec((step, 96, 128), lambda i: (i, 0, 0))
    coefs = pl.BlockSpec((48, 8), lambda i: (0, 0))
    damps = pl.BlockSpec((1, 128 * step), lambda i: (0, i))
    return pl.pallas_call(
        last_kernel,
        grid=(32 // step,),
        in_specs=[packed, half, half, packed, coefs, damps],
        out_specs=wide,
        out_shape=jax.ShapeDtypeStruct((2, 48, 4096), F32),
        name="add_last",
    )(part, below, above, pot, coef, damp)


ACROSS = (0, -1, 1, 2)


def grid_kernel(where_ref, own_ref, own_far_ref, other_ref, other_far_ref, v_ref, pot_ref, out_ref, x_ref, w_ref):
    y, core, x = (where_ref[i] for i in range(3))
    owners = [pl.ds(8 * lax.rem(x + across + 4, 4), 8) for across in ACROSS]
    for i, owner in enumerate(owners):
        for k in range(2):
            part = v_ref[owner, 48 * k : 48 * k + 48, :].reshape(384, 128)
            x_ref[384 * i : 384 * i + 384, 128 * k : 128 * k + 128] = part
    halves = (own_ref, own_far_ref), (other_ref, other_far_ref)
    for n, (half, c) in enumerate(zip(halves, (core, 1 - core))):
        for m, (t_ref, rows) in enumerate(zip(half, (y, 1 - y))):
            on_grid = dot(t_ref[...], x_ref[...])
            pot = pot_ref[:, 2 * rows + c].reshape(384, 128)
            weighted = jnp.concatenate([pot, pot], axis=1) * on_grid
            at = 768 * n + 384 * m
            w_ref[:, at : at + 384] = weighted.T.astype(BF16)
    for i, owner in enumerate(owners):
        at = slice(384 * i, 384 * i + 384)
        summed = 0.0
        for n, half in enumerate(halves):
            t = jnp.concatenate([t_ref[:, at] for t_ref in half], axis=0)
            summed = summed + dot(w_ref[:, 768 * n : 768 * n + 768], t)
        back = summed.T.astype(BF16)
        for k in range(2):
            out_ref[owner, 48 * k : 48 * k + 48, :] = back[:, 128 * k : 128 * k + 128].reshape(8, 48, 128)


def on_cells(where, table, v, pot):
    return pl.pallas_call(
        grid_kernel,
        in_specs=[SMEM] + [VMEM] * 6,
        out_specs=VMEM,
        out_shape=jax.ShapeDtypeStruct((32, 96, 128), BF16),
        scratch_shapes=[pltpu.VMEM((1536, 256), BF16), pltpu.VMEM((256, 1536), BF16)],
        compiler_params=PARAMS,
        name="on_cells",
    )(where, *table, v, pot)


def over_z(transform):
    columns = transform.shape[1] // 4
    block = lax.dynamic_slice_in_dim(transform, columns * lax.axis_index("x"), columns, 1)
    block = jnp.broadcast_to(block[None], (8,) + block.shape)
    return lax.all_to_all(block, "z", split_axis=0, concat_axis=0, tiled=True).reshape(-1, columns)


def over_x(block):
    return [lax.ppermute(block, "x", [(i, (i - across) % 4) for i in range(4)]) for across in ACROSS[1:]]


def over_plane(block):
    far = lax.ppermute(block, "y_lo", [(0, 1), (1, 0)])
    own, far, near = lax.optimization_barrier((block, far, over_x(block)))
    mine = jnp.concatenate([own] + near, axis=1)
    others = lax.optimization_barrier(over_x(far))
    mine = [mine, jnp.concatenate([far] + others, axis=1)]
    return mine + [lax.ppermute(rows, "core", [(0, 1), (1, 0)]) for rows in mine]


def regroup(x):
    return lax.all_to_all(x, GRID, split_axis=0, concat_axis=0, tiled=True)


def halos(first, last):
    size = 8
    up = [(i, i + 1) for i in range(size - 1)]
    down = [(j, i) for i, j in up]
    return lax.ppermute(last, HEL, up), lax.ppermute(first, HEL, down)


def coefficients(helicity, band, rotation, coupling):
    first = 2 * lax.axis_index(HEL)
    quantum = band.astype(F32)
    j_term = quantum * (quantum + 1.0)
    k_values = helicity.astype(F32)
    base = jnp.sqrt(jnp.maximum(j_term[:, None] - (k_values * (k_values + 1.0))[None, :], 0.0)) / JMAX
    linked = (helicity[1:] - helicity[:-1] == 1).astype(F32)
    linked = jnp.concatenate([linked, jnp.zeros((1,), F32)])
    coriolis = coupling[:, None] * base * linked[None, :]
    angular = rotation[:, None] * (j_term[:, None] - 2.0 * k_values * k_values) / (JMAX * JMAX)
    padded = jnp.concatenate([jnp.zeros_like(coriolis[:, :1]), coriolis], axis=1)
    part = lax.dynamic_slice_in_dim(padded, first, 3, 1)
    angular = lax.dynamic_slice_in_dim(angular, first, 2, 1)
    return jnp.concatenate(
        [angular, part[:, 1:2], part[:, 1:2], part[:, 0:1], part[:, 2:3], part[:, 0:2]], axis=1
    )


def local(
    phi_prev, phi_curr, helicity, band, rotation, coupling, damping, potential, transform, radial_long, radial_short
):
    where = jnp.stack([lax.axis_index(name) for name in ("y_lo", "core", "x")]).astype(jnp.int32)
    coef = coefficients(helicity, band, rotation, coupling)
    damp = damping.reshape(1, -1)
    cell_damp = lax.dynamic_slice_in_dim(damp, 128 * lax.axis_index(GRID), 128, 1)
    pot_cells = potential.reshape(8, 4, 48, 128)

    two_damp = 2.0 * damp.reshape(32, 1, 128)
    sides = jnp.concatenate([coef[:, 4], coef[:, 5]]).reshape(1, 96, 1)

    first, last = (pack((8192.0 * phi_curr[k]).astype(F16)) for k in range(2))
    below, above = lax.optimization_barrier(halos(first, last))
    block = over_z(transform)
    part, rounded = local_part(phi_curr, phi_prev, coef, damp, radial_long, radial_short)
    def add_beside(part, below, above):
        lower = part[:, :48] + two_damp * (sides[:, :48] * (below.astype(F32) / 8192))
        upper = part[:, 48:] + two_damp * (sides[:, 48:] * (above.astype(F32) / 8192))
        return lower, upper

    lower, upper = add_beside(part, below, above)
    sent = [(8192.0 * rounded.astype(F32)).astype(F16), (32.0 * lower).astype(F16), (32.0 * upper).astype(F16)]
    sent, part, below, above, _ = lax.optimization_barrier((jnp.concatenate(sent, axis=1), part, below, above, block))
    by_cells = regroup(sent)
    base = jnp.concatenate(add_beside(part, below, above), axis=1)
    table = over_plane(block)
    pot = on_cells(where, table, (by_cells[:, :96].astype(F32) / 8192).astype(BF16), pot_cells)
    next_cells = by_cells[:, 96:].astype(F32) / 32 + 2.0 * cell_damp * pot.astype(F32)
    first, last, pot = lax.optimization_barrier((sent[:, 96:144], sent[:, 144:], pot))
    pot_back = regroup(pot)
    pot_after = on_cells(where, table, next_cells.astype(BF16), pot_cells)
    below, above = halos(first, last)
    pot_after, below, above, base = lax.optimization_barrier((pot_after, below, above, base))
    pot_below, pot_above = halos(pot_back[:, :48], pot_back[:, 48:])
    phi_next, part = next_part(base, pot_back, phi_curr, coef, damp, radial_long, radial_short)
    below = below.astype(F32) / 32 + two_damp * pot_below.astype(F32)
    above = above.astype(F32) / 32 + two_damp * pot_above.astype(F32)
    phi_after = add_last(part, below, above, regroup(pot_after), coef, damp)
    return phi_next, phi_after


def solution(mesh):
    inner = Mesh(mesh.devices.reshape(2, 4, 8, 2, 2), HEL + GRID)
    in_specs = (
        P(HEL, GRID, None),
        P(HEL, GRID, None),
        P(),
        P(GRID),
        P(GRID),
        P(GRID),
        P(),
        P(None, GRID),
        P(GRID, None),
        P(),
        P(),
    )
    out_specs = (P(HEL, GRID, None), P(HEL, GRID, None))
    return jax.shard_map(local, mesh=inner, in_specs=in_specs, out_specs=out_specs, check_vma=False)
```

```python
import functools
import jax
import jax.numpy as jnp
from jax import lax
from jax.experimental import pallas as pl
from jax.experimental.pallas import tpu as pltpu
from jax.sharding import Mesh, PartitionSpec as P

JMAX = 48
HEL = ("y_hi", "x")
GRID = ("z", "y_lo", "core")
VMEM = pl.BlockSpec(memory_space=pltpu.VMEM)
SMEM = pl.BlockSpec(memory_space=pltpu.SMEM)
PARAMS = pltpu.CompilerParams(vmem_limit_bytes=48 << 20)
F32, BF16, F16 = jnp.float32, jnp.bfloat16, jnp.float16


def split(x):
    high = x.astype(BF16)
    return high, (x - high.astype(F32)).astype(BF16)


def dot(a, b):
    return jnp.dot(a, b, preferred_element_type=F32)


def pack(v):
    return v.reshape(48, 32, 128).transpose(1, 0, 2)


def local_kernel(prev_ref, coef_ref, damp_ref, long_ref, short_ref, *refs):
    if len(refs) == 5:
        (v_ref, out_ref, rounded_ref, z_ref, y_ref), pot_ref = refs, None
    else:
        base_ref, pot_ref, v_ref, out_ref, z_ref, y_ref = refs

    def load(k, j):
        at = pl.ds(pl.multiple_of(j * 128, 128), 128)
        rows = slice(48 * k, 48 * k + 48)
        if pot_ref is None:
            rounded_ref[j, rows, :] = v_ref[k, :, at].astype(BF16)
            return v_ref[k, :, at]
        v = base_ref[j, rows, :] + 2.0 * damp_ref[:, at] * pot_ref[j, rows, :].astype(F32)
        v_ref[k, :, at] = v
        return v

    def halves(matrix):
        high, low = split(0.5 * (matrix + matrix.T))
        top = jnp.concatenate([high, high], axis=1)
        return jnp.concatenate([top, jnp.concatenate([low, jnp.zeros_like(low)], axis=1)], axis=0)

    row, column = (lax.broadcasted_iota(jnp.int32, (128, 128), axis) // 32 for axis in range(2))
    short = jnp.concatenate([short_ref[...]] * 4, axis=1)
    short = jnp.where(row == column, jnp.concatenate([short] * 4, axis=0), 0.0)
    long_kin, short_kin = halves(long_ref[...]), halves(short)
    pad = jnp.zeros((32, 128), F32)

    def times(kin, one, two):
        high, low = split(jnp.concatenate([one, two], axis=1))
        both = dot(kin, jnp.concatenate([high, low], axis=0))
        return both[0:128] + both[128:256]

    def first(i, _):
        z = []
        for n in range(2):
            at = pl.ds(pl.multiple_of(i * 256 + n * 128, 128), 128)
            z.append(jnp.concatenate([load(0, 2 * i + n), load(1, 2 * i + n), pad], axis=0).T)
            z_ref[at, :] = z[n]
        y = times(short_kin, *z)
        for n in range(2):
            at = pl.ds(pl.multiple_of(i * 256 + n * 128, 128), 128)
            y_ref[at, :] = y[:, 128 * n : 128 * n + 128]
        return 0

    lax.fori_loop(0, 16, first, 0, unroll=4)

    def second(m, _):
        at = [pl.ds(2 * m + n, 128, stride=32) for n in range(2)]
        y = times(long_kin, z_ref[at[0], :], z_ref[at[1], :])
        for n in range(2):
            y_ref[at[n], :] = y_ref[at[n], :] + y[:, 128 * n : 128 * n + 128]
        return 0

    lax.fori_loop(0, 16, second, 0, unroll=4)

    def third(i, _):
        at = pl.ds(pl.multiple_of(i * 128, 128), 128)
        kinetic = y_ref[at, :].T
        damp = damp_ref[:, at]
        v0, v1 = v_ref[0, :, at], v_ref[1, :, at]
        h0 = kinetic[0:48] + coef_ref[:, 0:1] * v0 + coef_ref[:, 2:3] * v1
        h1 = kinetic[48:96] + coef_ref[:, 1:2] * v1 + coef_ref[:, 3:4] * v0
        out_ref[i, 0:48, :] = damp * (2.0 * h0 - damp * prev_ref[0, :, at])
        out_ref[i, 48:96, :] = damp * (2.0 * h1 - damp * prev_ref[1, :, at])
        return 0

    lax.fori_loop(0, 32, third, 0, unroll=4)


PACKED = jax.ShapeDtypeStruct((32, 96, 128), F32)
SCRATCH = [pltpu.VMEM((4096, 128), F32)] * 2


def local_part(v, prev, coef, damp, radial_long, radial_short):
    return pl.pallas_call(
        local_kernel,
        in_specs=[VMEM] * 6,
        out_specs=[VMEM, VMEM],
        out_shape=[PACKED, jax.ShapeDtypeStruct(PACKED.shape, BF16)],
        scratch_shapes=SCRATCH,
        compiler_params=PARAMS,
        name="local_part",
    )(prev, coef, damp, radial_long, radial_short, v)


def next_part(base, pot, prev, coef, damp, radial_long, radial_short):
    return pl.pallas_call(
        local_kernel,
        in_specs=[VMEM] * 7,
        out_specs=[VMEM, VMEM],
        out_shape=[jax.ShapeDtypeStruct(prev.shape, F32), PACKED],
        scratch_shapes=SCRATCH,
        compiler_params=PARAMS,
        name="next_part",
    )(prev, coef, damp, radial_long, radial_short, base, pot)


def last_kernel(part_ref, below_ref, above_ref, pot_ref, coef_ref, damp_ref, out_ref):
    for j in range(pot_ref.shape[0]):
        at = pl.ds(128 * j, 128)
        two_damp = 2.0 * damp_ref[:, at]
        pot0 = pot_ref[j, 0:48, :].astype(F32) + coef_ref[:, 4:5] * below_ref[j]
        pot1 = pot_ref[j, 48:96, :].astype(F32) + coef_ref[:, 5:6] * above_ref[j]
        out_ref[0, :, at] = part_ref[j, 0:48, :] + two_damp * pot0
        out_ref[1, :, at] = part_ref[j, 48:96, :] + two_damp * pot1


def add_last(part, below, above, pot, coef, damp):
    step = 16
    wide = pl.BlockSpec((2, 48, 128 * step), lambda i: (0, 0, i))
    half = pl.BlockSpec((step, 48, 128), lambda i: (i, 0, 0))
    packed = pl.BlockSpec((step, 96, 128), lambda i: (i, 0, 0))
    coefs = pl.BlockSpec((48, 8), lambda i: (0, 0))
    damps = pl.BlockSpec((1, 128 * step), lambda i: (0, i))
    return pl.pallas_call(
        last_kernel,
        grid=(32 // step,),
        in_specs=[packed, half, half, packed, coefs, damps],
        out_specs=wide,
        out_shape=jax.ShapeDtypeStruct((2, 48, 4096), F32),
        compiler_params=PARAMS,
        name="add_last",
    )(part, below, above, pot, coef, damp)


ACROSS = (0, -1, 1, 2)


def grid_kernel(where_ref, own_ref, own_far_ref, other_ref, other_far_ref, v_ref, pot_ref, out_ref, x_ref, w_ref):
    y, core, x = (where_ref[i] for i in range(3))
    owners = [pl.ds(8 * lax.rem(x + across + 4, 4), 8) for across in ACROSS]
    for i, owner in enumerate(owners):
        for k in range(2):
            part = v_ref[owner, 48 * k : 48 * k + 48, :].reshape(384, 128)
            x_ref[384 * i : 384 * i + 384, 128 * k : 128 * k + 128] = part
    halves = (own_ref, own_far_ref), (other_ref, other_far_ref)
    for n, (half, c) in enumerate(zip(halves, (core, 1 - core))):
        for m, (t_ref, rows) in enumerate(zip(half, (y, 1 - y))):
            on_grid = dot(t_ref[...], x_ref[...])
            pot = pot_ref[:, 2 * rows + c].reshape(384, 128)
            weighted = jnp.concatenate([pot, pot], axis=1) * on_grid
            at = 768 * n + 384 * m
            w_ref[:, at : at + 384] = weighted.T.astype(BF16)
    for i, owner in enumerate(owners):
        at = slice(384 * i, 384 * i + 384)
        summed = 0.0
        for n, half in enumerate(halves):
            t = jnp.concatenate([t_ref[:, at] for t_ref in half], axis=0)
            summed = summed + dot(w_ref[:, 768 * n : 768 * n + 768], t)
        back = summed.T.astype(BF16)
        for k in range(2):
            out_ref[owner, 48 * k : 48 * k + 48, :] = back[:, 128 * k : 128 * k + 128].reshape(8, 48, 128)


def on_cells(where, table, v, pot):
    return pl.pallas_call(
        grid_kernel,
        in_specs=[SMEM] + [VMEM] * 6,
        out_specs=VMEM,
        out_shape=jax.ShapeDtypeStruct((32, 96, 128), BF16),
        scratch_shapes=[pltpu.VMEM((1536, 256), BF16), pltpu.VMEM((256, 1536), BF16)],
        compiler_params=PARAMS,
        name="on_cells",
    )(where, *table, v, pot)


def over_z(transform):
    columns = transform.shape[1] // 4
    block = lax.dynamic_slice_in_dim(transform, columns * lax.axis_index("x"), columns, 1)
    block = jnp.broadcast_to(block[None], (8,) + block.shape)
    return lax.all_to_all(block, "z", split_axis=0, concat_axis=0, tiled=True).reshape(-1, columns)


def over_x(block):
    return [lax.ppermute(block, "x", [(i, (i - across) % 4) for i in range(4)]) for across in ACROSS[1:]]


def over_plane(block):
    far = lax.ppermute(block, "y_lo", [(0, 1), (1, 0)])
    own, far, near = lax.optimization_barrier((block, far, over_x(block)))
    mine = jnp.concatenate([own] + near, axis=1)
    others = lax.optimization_barrier(over_x(far))
    mine = [mine, jnp.concatenate([far] + others, axis=1)]
    return mine + [lax.ppermute(rows, "core", [(0, 1), (1, 0)]) for rows in mine]


def regroup(x):
    return lax.all_to_all(x, GRID, split_axis=0, concat_axis=0, tiled=True)


def halos(first, last):
    size = 8
    up = [(i, i + 1) for i in range(size - 1)]
    down = [(j, i) for i, j in up]
    return lax.ppermute(last, HEL, up), lax.ppermute(first, HEL, down)


def coefficients(helicity, band, rotation, coupling):
    first = 2 * lax.axis_index(HEL)
    quantum = band.astype(F32)
    j_term = quantum * (quantum + 1.0)
    k_values = helicity.astype(F32)
    base = jnp.sqrt(jnp.maximum(j_term[:, None] - (k_values * (k_values + 1.0))[None, :], 0.0)) / JMAX
    linked = (helicity[1:] - helicity[:-1] == 1).astype(F32)
    linked = jnp.concatenate([linked, jnp.zeros((1,), F32)])
    coriolis = coupling[:, None] * base * linked[None, :]
    angular = rotation[:, None] * (j_term[:, None] - 2.0 * k_values * k_values) / (JMAX * JMAX)
    padded = jnp.concatenate([jnp.zeros_like(coriolis[:, :1]), coriolis], axis=1)
    part = lax.dynamic_slice_in_dim(padded, first, 3, 1)
    angular = lax.dynamic_slice_in_dim(angular, first, 2, 1)
    return jnp.concatenate(
        [angular, part[:, 1:2], part[:, 1:2], part[:, 0:1], part[:, 2:3], part[:, 0:2]], axis=1
    )


def local(
    phi_prev, phi_curr, helicity, band, rotation, coupling, damping, potential, transform, radial_long, radial_short
):
    where = jnp.stack([lax.axis_index(name) for name in ("y_lo", "core", "x")]).astype(jnp.int32)
    coef = coefficients(helicity, band, rotation, coupling)
    damp = damping.reshape(1, -1)
    cell_damp = lax.dynamic_slice_in_dim(damp, 128 * lax.axis_index(GRID), 128, 1)
    pot_cells = potential.reshape(8, 4, 48, 128)

    two_damp = 2.0 * damp.reshape(32, 1, 128)
    sides = jnp.concatenate([coef[:, 4], coef[:, 5]]).reshape(1, 96, 1)

    first, last = (pack((8192.0 * phi_curr[k]).astype(F16)) for k in range(2))
    below, above = lax.optimization_barrier(halos(first, last))
    block = over_z(transform)
    part, rounded = local_part(phi_curr, phi_prev, coef, damp, radial_long, radial_short)
    def add_beside(part, below, above):
        lower = part[:, :48] + two_damp * (sides[:, :48] * (below.astype(F32) / 8192))
        upper = part[:, 48:] + two_damp * (sides[:, 48:] * (above.astype(F32) / 8192))
        return lower, upper

    lower, upper = add_beside(part, below, above)
    sent = [(8192.0 * rounded.astype(F32)).astype(F16), (32.0 * lower).astype(F16), (32.0 * upper).astype(F16)]
    sent, part, below, above, _ = lax.optimization_barrier((jnp.concatenate(sent, axis=1), part, below, above, block))
    by_cells = regroup(sent)
    base = jnp.concatenate(add_beside(part, below, above), axis=1)
    table = over_plane(block)
    pot = on_cells(where, table, (by_cells[:, :96].astype(F32) / 8192).astype(BF16), pot_cells)
    next_cells = by_cells[:, 96:].astype(F32) / 32 + 2.0 * cell_damp * pot.astype(F32)
    sent, pot = lax.optimization_barrier((sent, pot))
    pot_back = regroup(pot)
    pot_after = on_cells(where, table, next_cells.astype(BF16), pot_cells)
    below, above = halos(sent[:, 96:144], sent[:, 144:])
    pot_after, below, above, base = lax.optimization_barrier((pot_after, below, above, base))
    pot_below, pot_above = halos(pot_back[:, :48], pot_back[:, 48:])
    phi_next, part = next_part(base, pot_back, phi_curr, coef, damp, radial_long, radial_short)
    below = below.astype(F32) / 32 + two_damp * pot_below.astype(F32)
    above = above.astype(F32) / 32 + two_damp * pot_above.astype(F32)
    phi_after = add_last(part, below, above, regroup(pot_after), coef, damp)
    return phi_next, phi_after


def solution(mesh):
    inner = Mesh(mesh.devices.reshape(2, 4, 8, 2, 2), HEL + GRID)
    in_specs = (
        P(HEL, GRID, None),
        P(HEL, GRID, None),
        P(),
        P(GRID),
        P(GRID),
        P(GRID),
        P(),
        P(None, GRID),
        P(GRID, None),
        P(),
        P(),
    )
    out_specs = (P(HEL, GRID, None), P(HEL, GRID, None))
    return jax.shard_map(local, mesh=inner, in_specs=in_specs, out_specs=out_specs, check_vma=False)
```
